32 devices in a mesh: dp: 4 (over y, x), row: 2 (over core), col: 4 (over z).
Axes of the slice: x: 2, y: 2, z: 4, core: 2. Of those that a mesh axis runs over, the one named last changes fastest.
Arguments:
- inputs: bfloat16 [4096, 1024], P(('dp', 'col'), 'row'), may hold values from -6 to 6
- norm_in: float32 [1, 1024], P(None, 'row'), may hold values from 0.1 to 1.9
- w_proj: bfloat16 [1, 1024, 8, 768], P(None, 'row', 'col'), may hold values from -0.1875 to 0.1875
- w_small: bfloat16 [1, 1024, 8, 2], P(None, 'row', 'col'), may hold values from -0.1875 to 0.1875
- w_conv: float32 [1, 4, 8, 512], P(None, None, 'col'), may hold values from -3 to 3
- a_log: float32 [1, 8], P(None, 'col'), may hold values from -3 to 1.5
- dt_bias: float32 [1, 8], P(None, 'col'), may hold values from -4 to -1
- norm_out: float32 [1, 256], replicated, may hold values from 0.1 to 1.9
- w_out: bfloat16 [1, 8, 256, 1024], P(None, 'col', None, 'row'), may hold values from -0.25 to 0.25
- norm_ffn: float32 [1, 1024], P(None, 'row'), may hold values from 0.1 to 1.9
- w_gu: bfloat16 [1, 1024, 2, 2816], P(None, 'row', None, 'col'), may hold values from -0.1875 to 0.1875
- w_down: bfloat16 [1, 2816, 1024], P(None, 'col', 'row'), may hold values from -0.21875 to 0.21875
- block_resets: int32 [4, 16], P('dp'), may hold values 0 or 1
- cotangent: bfloat16 [4096, 1024], P(('dp', 'col'), 'row'), may hold values from -6 to 6
Outputs:
- result: bfloat16 [4096, 1024], P(('dp', 'col'), 'row')
- grad_inputs: float32 [4096, 1024], P(('dp', 'col'), 'row')
- grad_norm_in: float32 [1, 1024], P(None, 'row')
- grad_w_proj: float32 [1, 1024, 8, 768], P(None, 'row', 'col')
- grad_w_small: float32 [1, 1024, 8, 2], P(None, 'row', 'col')
- grad_w_conv: float32 [1, 4, 8, 512], P(None, None, 'col')
- grad_a_log: float32 [1, 8], P(None, 'col')
- grad_dt_bias: float32 [1, 8], P(None, 'col')
- grad_norm_out: float32 [1, 256], replicated
- grad_w_out: float32 [1, 8, 256, 1024], P(None, 'col', None, 'row')
- grad_norm_ffn: float32 [1, 1024], P(None, 'row')
- grad_w_gu: float32 [1, 1024, 2, 2816], P(None, 'row', None, 'col')
- grad_w_down: float32 [1, 2816, 1024], P(None, 'col', 'row')
The draws below stay inside these ranges and needn't reach their ends.
Inputs may be any that keep to these rules, and one draw needn't show every extreme that they name: `block_resets`: 1 marks a block of 64 tokens at which a new segment begins; the first block of every sequence begins one whatever its entry.
All inputs are finite; a program needn't handle non-finite values.
Results may differ from the reference program's by a relative error of at most 0.01505.
Values may be sent and summed in bfloat16 or wider, within the bound.
A program may use at most 128 MiB of HBM per device.

```python
import jax
import jax.numpy as jnp
from jax import lax

D = 1024
H = 8
DV = 256
FF = 2816
CONV = 4
BLOCK = 64
LAYERS = 1
SEQ_LEN = 1024
SEQS = 4
TOKENS = 4096
BLOCKS = 16
PROJ = 768
CHANNELS = 512


def place_ends(entries, key, smallest, top_value):
    place = [jax.random.randint(jax.random.fold_in(key, axis), (), 0, length) for axis, length in enumerate(entries.shape)]
    main_axis = entries.shape.index(max(entries.shape))
    neighbour = place[:main_axis] + [(place[main_axis] + 1) % entries.shape[main_axis]] + place[main_axis + 1:]
    return entries.at[tuple(place)].set(smallest).at[tuple(neighbour)].set(top_value)


def shard_levels(stream_key, shape, cuts, low, largest):
    level = 1.0
    for axis_at, blocks in cuts:
        steps = jax.random.uniform(jax.random.fold_in(jax.random.fold_in(stream_key, 6), axis_at), (blocks,), jnp.float32, low / len(cuts), largest / len(cuts))
        level = level * jnp.repeat(jnp.exp(steps), shape[axis_at] // blocks).reshape((-1,) + (1,) * (len(shape) - 1 - axis_at))
    return level


def noise(own_key, extent, scale, most, cuts=(), kind=jnp.bfloat16):
    array = jax.random.normal(own_key, extent, jnp.float32) * scale
    if len(cuts) > 0:
        array = shard_levels(own_key, extent, cuts, -0.22, 0.18) * array
    return jnp.clip(array, min=-most, max=most).astype(kind)


def setup_inputs(seed: int = 0) -> dict:
    keys = jax.random.split(jax.random.key(seed), 15)
    return {
        "inputs": noise(keys[0], (TOKENS, D), 1.0, 6.0, ((0, 16), (1, 2))),
        "norm_in": jnp.clip(1.0 + 0.18 * jax.random.normal(keys[1], (LAYERS, D), jnp.float32), 0.1, 1.9),
        "w_proj": noise(keys[2], (LAYERS, D, H, PROJ), D ** -0.5, 0.1875, ((1, 2), (2, 4))),
        "w_small": noise(keys[3], (LAYERS, D, H, 2), D ** -0.5, 0.1875, ((1, 2), (2, 4))),
        "w_conv": noise(keys[4], (LAYERS, CONV, H, CHANNELS), CONV ** -0.5, 3.0, ((2, 4),), jnp.float32),
        "a_log": jnp.clip(-3.0 + 4.5 * jax.random.uniform(keys[5], (LAYERS, H), jnp.float32) ** shard_levels(keys[5], (LAYERS, H), ((1, 4),), -0.2, 0.2), -3.0, 1.5),
        "dt_bias": jnp.clip(-4.0 + 3.0 * jax.random.uniform(keys[6], (LAYERS, H), jnp.float32) ** shard_levels(keys[6], (LAYERS, H), ((1, 4),), -0.2, 0.2), -4.0, -1.0),
        "norm_out": jnp.clip(1.0 + 0.18 * jax.random.normal(keys[7], (LAYERS, DV), jnp.float32), 0.1, 1.9),
        "w_out": noise(keys[8], (LAYERS, H, DV, D), (H * DV // 4) ** -0.5, 0.25, ((1, 4), (3, 2))),
        "norm_ffn": jnp.clip(1.0 + 0.18 * jax.random.normal(keys[9], (LAYERS, D), jnp.float32), 0.1, 1.9),
        "w_gu": noise(keys[10], (LAYERS, D, 2, FF), D ** -0.5, 0.1875, ((1, 2), (3, 4))),
        "w_down": noise(keys[11], (LAYERS, FF, D), (FF // 4) ** -0.5, 0.21875, ((1, 4), (2, 2))),
        "block_resets": place_ends((jax.random.randint(keys[12], (SEQS, BLOCKS), 0, 4) < 1).astype(jnp.int32), jax.random.fold_in(keys[12], 1), 0, 1),
        "cotangent": noise(keys[13], (TOKENS, D), 1.0, 6.0, ((0, 16), (1, 2))),
    }


norm_eps = 1e-05
unit_eps = 1e-06
precise = lax.Precision.HIGHEST

@jax.custom_vjp
def low(v):
    return lax.optimization_barrier(v.astype(jnp.bfloat16)).astype(jnp.float32)

@jax.custom_vjp
def low_back(v):
    return v

def low_keep(v):
    return (low(v), None)

def low_pass(kept, grad):
    return (grad,)

def back_keep(v):
    return (v, None)

def back_low(kept, grad):
    return (low(grad),)
low.defvjp(low_keep, low_pass)
low_back.defvjp(back_keep, back_low)

def block_flags(block_resets):
    column = lax.broadcasted_iota(jnp.int32, block_resets.shape, 1)
    return jnp.where(column == 0, 1, block_resets).reshape(-1).astype(jnp.int32)

def conv_silu(inputs, weights, segment):
    tap_count = weights.shape[0]
    length = inputs.shape[0]
    padded = jnp.concatenate([jnp.zeros((tap_count - 1, inputs.shape[1]), jnp.float32), inputs], 0)
    seg_padded = jnp.concatenate([jnp.full((tap_count - 1,), -1, jnp.int32), segment], 0)
    summed = jnp.zeros_like(inputs)
    for offset in range(tap_count):
        first_row = tap_count - 1 - offset
        shifted = lax.slice_in_dim(padded, first_row, first_row + length, axis=0)
        same_seg = (lax.slice_in_dim(seg_padded, first_row, first_row + length, axis=0) == segment).astype(jnp.float32)
        summed = summed + weights[offset] * shifted * same_seg[:, None]
    return jax.nn.silu(summed)

def block_step(carried, pieces):
    queries, keys_now, values, log_decay, beta_rows, reset_now = pieces
    carried = carried * (1.0 - reset_now)
    cumulative = jnp.cumsum(log_decay)
    decays = jnp.exp(cumulative)
    block_size = log_decay.shape[0]
    row_ids = lax.broadcasted_iota(jnp.int32, (block_size, block_size), 0)
    col_ids = lax.broadcasted_iota(jnp.int32, (block_size, block_size), 1)
    lower_incl = row_ids >= col_ids
    lower_strict = row_ids > col_ids
    spread = cumulative[:, None] - cumulative[None, :]
    within = jnp.where(lower_incl, jnp.exp(jnp.where(lower_incl, spread, 0.0)), 0.0)
    key_key = jnp.dot(keys_now, keys_now.T, precision=precise)
    coupling = jnp.where(lower_strict, beta_rows[:, None] * key_key * within, 0.0)
    system = jnp.eye(block_size, dtype=jnp.float32) + coupling
    value_width = values.shape[1]
    targets = jnp.concatenate([beta_rows[:, None] * values, (beta_rows * decays)[:, None] * keys_now], 1)
    solved = lax.linalg.triangular_solve(system, targets, left_side=True, lower=True, unit_diagonal=True)
    updates = solved[:, :value_width] - jnp.dot(solved[:, value_width:], carried, precision=precise)
    scores = jnp.dot(queries, keys_now.T, precision=precise) * within
    output = jnp.dot(queries * decays[:, None], carried, precision=precise) + jnp.dot(scores, updates, precision=precise)
    remaining = jnp.exp(cumulative[-1] - cumulative)
    new_state = decays[-1] * carried + jnp.dot((keys_now * remaining[:, None]).T, updates, precision=precise)
    return (new_state, output)

def delta_rule(queries, keys_all, values, log_decay, beta_rows, reset_flags):
    length = queries.shape[0]
    blocks = length // BLOCK

    def to_blocks(source):
        return source.reshape((blocks, BLOCK) + source.shape[1:])
    initial = jnp.zeros((keys_all.shape[1], values.shape[1]), jnp.float32)
    final_state, outputs = lax.scan(jax.checkpoint(block_step), initial, (to_blocks(queries), to_blocks(keys_all), to_blocks(values), to_blocks(log_decay), to_blocks(beta_rows), reset_flags.astype(jnp.float32)))
    return outputs.reshape(length, values.shape[1])

def mixer_head(projected, small_proj, conv_weights, a_log, dt_bias, gain_out, reset_flags):
    segment = jnp.repeat(jnp.cumsum(reset_flags).astype(jnp.int32), BLOCK)
    channels = conv_weights.shape[1]
    value_width = gain_out.shape[0]
    key_width = (channels - value_width) // 2
    mixed_out = conv_silu(projected[:, :channels], conv_weights, segment)
    queries = mixed_out[:, :key_width]
    keys_all = mixed_out[:, key_width:2 * key_width]
    values = mixed_out[:, 2 * key_width:]
    queries = queries * lax.rsqrt(lax.optimization_barrier(jnp.sum(queries * queries, -1, keepdims=True)) + unit_eps) * key_width ** (-0.5)
    keys_all = keys_all * lax.rsqrt(lax.optimization_barrier(jnp.sum(keys_all * keys_all, -1, keepdims=True)) + unit_eps)
    beta_rows = jax.nn.sigmoid(small_proj[:, 0])
    log_decay = -jnp.exp(a_log) * jax.nn.softplus(small_proj[:, 1] + dt_bias)
    output = delta_rule(queries, keys_all, values, log_decay, beta_rows, reset_flags)
    gate_rows = projected[:, channels:]
    return output * lax.rsqrt(lax.optimization_barrier(jnp.mean(output * output, -1, keepdims=True)) + norm_eps) * gain_out * jax.nn.silu(gate_rows)

def mixer_heads(projected, small_proj, conv_weights, a_log, dt_bias, gain_out, reset_flags):
    return jax.vmap(mixer_head, in_axes=(1, 1, 1, 0, 0, None, None), out_axes=1)(projected, small_proj, conv_weights, a_log, dt_bias, gain_out, reset_flags)

def norm_rows(residual, gain_row):
    return residual * lax.rsqrt(lax.optimization_barrier(jnp.mean(residual * residual, -1, keepdims=True)) + norm_eps) * gain_row

def layer_forward(residual, layer_weights, reset_flags):
    gain_in, proj_weight, small_weight, conv_weight, decay_log, decay_bias, gain_out, out_weight, gain_ffn, gate_up_weight, down_weight = layer_weights
    length = residual.shape[0]
    head_count = proj_weight.shape[1]
    normed = low(norm_rows(residual, gain_in))
    projected = low_back(jnp.dot(normed, proj_weight.reshape(proj_weight.shape[0], -1), precision=precise)).reshape(length, head_count, -1)
    small_proj = low_back(jnp.dot(normed, small_weight.reshape(small_weight.shape[0], -1), precision=precise)).reshape(length, head_count, -1)
    mixed_out = low(mixer_heads(projected, small_proj, conv_weight, decay_log, decay_bias, gain_out, reset_flags))
    branch = low_back(jnp.dot(mixed_out.reshape(length, -1), out_weight.reshape(-1, out_weight.shape[-1]), precision=precise))
    residual = residual + branch
    normed = low(norm_rows(residual, gain_ffn))
    gate_up = low_back(jnp.einsum('td,dkf->tkf', normed, gate_up_weight, precision=precise))
    hidden = low(jax.nn.silu(gate_up[:, 0]) * gate_up[:, 1])
    branch = low_back(jnp.dot(hidden, down_weight, precision=precise))
    return residual + branch

def reference(inputs, norm_in, w_proj, w_small, w_conv, a_log, dt_bias, norm_out, w_out, norm_ffn, w_gu, w_down, block_resets, cotangent):
    weights = (norm_in.astype(jnp.float32), w_proj.astype(jnp.float32), w_small.astype(jnp.float32), w_conv.astype(jnp.float32), a_log.astype(jnp.float32), dt_bias.astype(jnp.float32), norm_out.astype(jnp.float32), w_out.astype(jnp.float32), norm_ffn.astype(jnp.float32), w_gu.astype(jnp.float32), w_down.astype(jnp.float32))
    residual_all = inputs.astype(jnp.float32).reshape(SEQS, SEQ_LEN, D)
    cot_all = cotangent.astype(jnp.float32).reshape(SEQS, SEQ_LEN, D)

    def one_sequence(totals, pieces):
        residual, cot_rows, reset_row = pieces
        reset_flags = block_flags(reset_row[None, :])

        def forward(start_rows, all_weights):
            current = start_rows
            for layer_index in range(LAYERS):
                current = layer_forward(current, tuple((weight[layer_index] for weight in all_weights)), reset_flags)
            return current
        result, pullback = jax.vjp(forward, residual, weights)
        grad_rows, grad_weights = pullback(cot_rows)
        totals = jax.tree.map(jnp.add, totals, grad_weights)
        return (totals, (result, grad_rows))
    initial = jax.tree.map(jnp.zeros_like, weights)
    totals, outputs = lax.scan(one_sequence, initial, (residual_all, cot_all, block_resets))
    results, grad_rows = outputs
    return (results.reshape(TOKENS, D).astype(jnp.bfloat16), grad_rows.reshape(TOKENS, D), totals[0], totals[1], totals[2], totals[3], totals[4], totals[5], totals[6], totals[7], totals[8], totals[9], totals[10])
```

```python
import jax
import jax.numpy as jnp
from jax import lax
from jax.experimental import pallas as pl
from jax.experimental.pallas import tpu as pltpu
from jax.sharding import PartitionSpec as P

BLOCK = 64
norm_eps = 1e-05
unit_eps = 1e-06


def block_flags(block_resets):
    column = lax.broadcasted_iota(jnp.int32, block_resets.shape, 1)
    return jnp.where(column == 0, 1, block_resets).reshape(-1)


SUPER = 256


def contract(left, right, left_dim, right_dim):
    dims = (((left_dim,), (right_dim,)), ((), ()))
    left_hi = left.astype(jnp.bfloat16)
    right_hi = right.astype(jnp.bfloat16)
    left_lo = (left - left_hi.astype(jnp.float32)).astype(jnp.bfloat16)
    right_lo = (right - right_hi.astype(jnp.float32)).astype(jnp.bfloat16)

    def single(one, other):
        return lax.dot_general(one, other, dims, preferred_element_type=jnp.float32)

    return single(left_hi, right_hi) + (single(left_hi, right_lo) + single(left_lo, right_hi))


@jax.custom_vjp
def nn(left, right):
    return contract(left, right, 1, 0)


@jax.custom_vjp
def nt(left, right):
    return contract(left, right, 1, 1)


@jax.custom_vjp
def tn(left, right):
    return contract(left, right, 0, 0)


nn.defvjp(lambda a, b: (nn(a, b), (a, b)), lambda k, g: (nt(g, k[1]), tn(k[0], g)))
nt.defvjp(lambda a, b: (nt(a, b), (a, b)), lambda k, g: (nn(g, k[1]), tn(g, k[0])))
tn.defvjp(lambda a, b: (tn(a, b), (a, b)), lambda k, g: (nt(k[1], g), nn(k[0], g)))


@jax.custom_vjp
def solve(inverse, coupling, targets):
    return nn(inverse, targets)


def solve_fwd(inverse, coupling, targets):
    solved = nn(inverse, targets)
    return solved, (inverse, solved)


def solve_bwd(kept, grad):
    inverse, solved = kept
    grad_targets = tn(inverse, grad)
    return jnp.zeros_like(inverse), -nt(grad_targets, solved), grad_targets


solve.defvjp(solve_fwd, solve_bwd)


def block_masks():
    rows = lax.broadcasted_iota(jnp.int32, (SUPER, SUPER), 0)
    cols = lax.broadcasted_iota(jnp.int32, (SUPER, SUPER), 1)
    shift = BLOCK.bit_length() - 1
    same = (rows >> shift) == (cols >> shift)
    return rows, cols, same


def unit_lower_inverse(coupling, rows, cols):
    eye = jnp.where(rows == cols, 1.0, 0.0)
    inverse = None
    for level in range(BLOCK.bit_length() - 1):
        pair = ((rows >> (level + 1)) == (cols >> (level + 1))) & (
            ((rows >> level) & 1) > ((cols >> level) & 1)
        )
        corner = jnp.where(pair, coupling, 0.0)
        if inverse is None:
            inverse = eye - corner
        else:
            inverse = inverse - nn(nn(inverse, corner), inverse)
    return inverse


def intra(query_act, key_act, values, beta, log_decay, inverse, masks):
    rows, cols, same = masks
    key_width = query_act.shape[1]
    queries = (
        query_act
        * lax.rsqrt(jnp.sum(query_act * query_act, -1, keepdims=True) + unit_eps)
        * key_width ** (-0.5)
    )
    keys_all = key_act * lax.rsqrt(jnp.sum(key_act * key_act, -1, keepdims=True) + unit_eps)
    eye = jnp.where(rows == cols, 1.0, 0.0)
    upto = jnp.where(same & (rows <= cols), 1.0, 0.0)
    sames = jnp.where(same, 1.0, 0.0)
    lower = same & (rows >= cols)
    strict = same & (rows > cols)
    cum_row = jnp.sum(log_decay * upto, 0, keepdims=True)
    total_row = jnp.sum(log_decay * sames, 0, keepdims=True)
    cum = jnp.sum(cum_row * eye, 1, keepdims=True)
    total = jnp.sum(total_row * eye, 1, keepdims=True)
    decays = jnp.exp(cum)
    within = jnp.where(lower, jnp.exp(jnp.where(lower, cum - cum_row, 0.0)), 0.0)
    coupling = jnp.where(strict, beta * nt(keys_all, keys_all) * within, 0.0)
    if inverse is None:
        inverse = unit_lower_inverse(coupling, rows, cols)
    solved_v = solve(inverse, coupling, beta * values)
    solved_k = solve(inverse, coupling, (beta * decays) * keys_all)
    scores = nt(queries, keys_all) * within
    return (
        solved_v,
        solved_k,
        scores,
        queries * decays,
        keys_all * jnp.exp(total - cum),
        jnp.exp(total),
    ), inverse


def gated(output, gate, gain):
    scaled = output * lax.rsqrt(jnp.mean(output * output, -1, keepdims=True) + norm_eps)
    return scaled * gain * (gate * lax.logistic(gate))


def gates(small, a_log, dt_bias):
    beta = lax.logistic(small[:, 0:1])
    shifted = small[:, 1:2] + dt_bias
    soft = jnp.maximum(shifted, 0.0) + jnp.log1p(jnp.exp(-jnp.abs(shifted)))
    return beta, -jnp.exp(a_log) * soft, shifted


def fill_padded(padded, projected_ref, channels):
    padded[0:8, :] = jnp.zeros((8, channels), jnp.float32)
    padded[8:, :] = projected_ref[:, :channels]


def taps_kept(reset_rows, offset):
    place = lax.broadcasted_iota(jnp.int32, reset_rows.shape, 0) & (BLOCK - 1)
    return jnp.where(place < offset, 1.0 - reset_rows, 1.0)


def convolve(padded, conv_ref, reset_rows, first):
    summed = None
    for offset in range(conv_ref.shape[0]):
        term = conv_ref[offset : offset + 1, :] * padded[pl.ds(8 + first - offset, SUPER), :]
        if offset:
            term = term * taps_kept(reset_rows, offset)
        summed = term if summed is None else summed + term
    return summed


def forward_kernel(
    projected_ref, small_ref, reset_ref, conv_ref, alog_ref, bias_ref, gain_ref,
    mixed_ref, output_ref, inverse_ref, state_ref, update_ref, padded,
):
    length = projected_ref.shape[0]
    channels = conv_ref.shape[1]
    value_width = gain_ref.shape[1]
    key_width = (channels - value_width) // 2
    masks = block_masks()
    fill_padded(padded, projected_ref, channels)
    pieces = []
    for first in range(0, length, SUPER):
        span = slice(first, first + SUPER)
        summed = convolve(padded, conv_ref, reset_ref[span, :], first)
        act = summed * lax.logistic(summed)
        beta, log_decay, _ = gates(small_ref[span, :], alog_ref[...], bias_ref[...])
        made, inverse = intra(
            act[:, :key_width], act[:, key_width : 2 * key_width], act[:, 2 * key_width :],
            beta, log_decay, None, masks,
        )
        inverse_ref[span, :] = inverse
        pieces.append(made)
    state = jnp.zeros((key_width, value_width), jnp.float32)
    for index, first in enumerate(range(0, length, SUPER)):
        solved_v, solved_k, scores, query_decay, key_rest, last = pieces[index]
        updates, reads = [], []
        for start in range(0, SUPER, BLOCK):
            part = slice(start, start + BLOCK)
            block = (first + start) // BLOCK
            reset_now = reset_ref[first + start : first + start + 1, :]
            state = state * (1.0 - reset_now)
            state_ref[block * key_width : (block + 1) * key_width, :] = state
            transfer = tn(key_rest[part], solved_k[part])
            added = tn(key_rest[part], solved_v[part])
            updates.append(solved_v[part] - nn(solved_k[part], state))
            reads.append(nn(query_decay[part], state))
            state = last[start : start + 1, :] * state + added - nn(transfer, state)
        update = jnp.concatenate(updates, 0)
        output = jnp.concatenate(reads, 0) + nn(scores, update)
        span = slice(first, first + SUPER)
        update_ref[span, :] = update
        output_ref[span, :] = output
        mixed_ref[span, :] = gated(output, projected_ref[span, channels:], gain_ref[...]).astype(
            mixed_ref.dtype
        )


def backward_kernel(
    projected_ref, small_ref, reset_ref, conv_ref, alog_ref, bias_ref, gain_ref,
    output_ref, inverse_ref, state_ref, update_ref, grad_ref,
    dproj_ref, dsmall_ref, dconv_ref, dalog_ref, dbias_ref, dgain_ref, padded, dpadded,
):
    length = projected_ref.shape[0]
    channels = conv_ref.shape[1]
    value_width = gain_ref.shape[1]
    key_width = (channels - value_width) // 2
    tap_count = conv_ref.shape[0]
    masks = block_masks()
    fill_padded(padded, projected_ref, channels)
    dpadded[length:, :] = jnp.zeros((8, channels), jnp.float32)
    dstate = jnp.zeros((key_width, value_width), jnp.float32)
    dgain = jnp.zeros((1, value_width), jnp.float32)
    dalog = jnp.zeros((1, 1), jnp.float32)
    dbias = jnp.zeros((1, 1), jnp.float32)
    dconv = [jnp.zeros((1, channels), jnp.float32) for _ in range(tap_count)]
    for first in reversed(range(0, length, SUPER)):
        span = slice(first, first + SUPER)
        _, pull_gated = jax.vjp(
            gated, output_ref[span, :], projected_ref[span, channels:], gain_ref[...]
        )
        doutput, dgate, dgain_part = pull_gated(grad_ref[span, :].astype(jnp.float32))
        dgain = dgain + dgain_part
        dproj_ref[span, channels:] = dgate.astype(dproj_ref.dtype)
        summed = convolve(padded, conv_ref, reset_ref[span, :], first)
        gate_of = lax.logistic(summed)
        act = summed * gate_of
        beta, log_decay, shifted = gates(small_ref[span, :], alog_ref[...], bias_ref[...])
        inverse = inverse_ref[span, :]
        made, pull_intra = jax.vjp(
            lambda q, k, v, b, g: intra(q, k, v, b, g, inverse, masks)[0],
            act[:, :key_width], act[:, key_width : 2 * key_width], act[:, 2 * key_width :],
            beta, log_decay,
        )
        _, solved_k, scores, query_decay, key_rest, last = made
        update = update_ref[span, :]
        dscores = nt(doutput, update)
        through = tn(scores, doutput)
        dupdates, dsolved_k, dquery, dkey, dlast = [], [], [], [], []
        for start in reversed(range(0, SUPER, BLOCK)):
            part = slice(start, start + BLOCK)
            block = (first + start) // BLOCK
            reset_now = reset_ref[first + start : first + start + 1, :]
            state = state_ref[block * key_width : (block + 1) * key_width, :]
            last_now = last[start : start + 1, :]
            transfer = tn(solved_k[part], key_rest[part])
            given = tn(query_decay[part], doutput[part]) - tn(solved_k[part], through[part])
            dupdate = through[part] + nn(key_rest[part], dstate)
            dupdates.append(dupdate)
            dsolved_k.append(-nt(dupdate, state))
            dquery.append(nt(doutput[part], state))
            dkey.append(nt(update[part], dstate))
            inner = jnp.sum(
                jnp.sum(state * dstate, 1, keepdims=True), 0, keepdims=True
            )
            place = lax.broadcasted_iota(jnp.int32, (BLOCK, 1), 0)
            dlast.append(jnp.where(place == 0, inner, 0.0))
            dstate = (last_now * dstate + given - nn(transfer, dstate)) * (1.0 - reset_now)
        joined = [jnp.concatenate(p[::-1], 0) for p in (dupdates, dsolved_k, dquery, dkey, dlast)]
        dq, dk, dv, dbeta, dlog = pull_intra(
            (joined[0], joined[1], dscores, joined[2], joined[3], joined[4])
        )
        dsmall_ref[span, 0:1] = dbeta * beta * (1.0 - beta)
        dshift = dlog * (-jnp.exp(alog_ref[...])) * lax.logistic(shifted)
        dsmall_ref[span, 1:2] = dshift
        dalog = dalog + jnp.sum(dlog * log_decay, 0, keepdims=True)
        dbias = dbias + jnp.sum(dshift, 0, keepdims=True)
        slope = gate_of * (1.0 + summed * (1.0 - gate_of))
        dpadded[span, :] = jnp.concatenate([dq, dk, dv], 1) * slope
    for first in range(0, length, SUPER):
        span = slice(first, first + SUPER)
        here = dpadded[span, :]
        total = conv_ref[0:1, :] * here
        dconv[0] = dconv[0] + jnp.sum(here * padded[pl.ds(8 + first, SUPER), :], 0, keepdims=True)
        place = lax.broadcasted_iota(jnp.int32, (SUPER, 1), 0)
        at_last = place >= SUPER - 8
        for offset in range(1, tap_count):
            back = padded[pl.ds(8 + first - offset, SUPER), :] * taps_kept(reset_ref[span, :], offset)
            dconv[offset] = dconv[offset] + jnp.sum(here * back, 0, keepdims=True)
            ahead = dpadded[pl.ds(first + offset, SUPER), :]
            kept = next_kept(reset_ref, first, length, offset)
            total = total + conv_ref[offset : offset + 1, :] * (ahead * kept)
        dproj_ref[span, :channels] = total.astype(dproj_ref.dtype)
    for offset in range(tap_count):
        dconv_ref[offset : offset + 1, :] = dconv[offset]
    dalog_ref[...] = dalog
    dbias_ref[...] = dbias
    dgain_ref[...] = dgain


def next_kept(reset_ref, first, length, offset):
    place = lax.broadcasted_iota(jnp.int32, (BLOCK, 1), 0)
    kept = []
    for start in range(first, first + SUPER, BLOCK):
        if start + BLOCK < length:
            after = 1.0 - reset_ref[start + BLOCK : start + 2 * BLOCK, :]
        else:
            after = jnp.zeros((BLOCK, 1), jnp.float32)
        kept.append(jnp.where(place + offset >= BLOCK, after, 1.0))
    return jnp.concatenate(kept, 0)


vmem_limit = 60 * 1024 * 1024


def run_kernel(kernel, out_shape, scratch, operands, cost):
    return pl.pallas_call(
        kernel,
        out_shape=out_shape,
        in_specs=[pl.BlockSpec(memory_space=pltpu.VMEM)] * len(operands),
        out_specs=[pl.BlockSpec(memory_space=pltpu.VMEM)] * len(out_shape),
        scratch_shapes=scratch,
        compiler_params=pltpu.CompilerParams(vmem_limit_bytes=vmem_limit),
        cost_estimate=pl.CostEstimate(flops=cost, bytes_accessed=8_000_000, transcendentals=1_000_000),
    )(*operands)


def head_forward(operands):
    projected, conv, gain = operands[0], operands[3], operands[6]
    length, value_width = projected.shape[0], gain.shape[1]
    key_width = (conv.shape[1] - value_width) // 2
    f32 = jnp.float32
    out_shape = [
        jax.ShapeDtypeStruct((length, value_width), jnp.bfloat16),
        jax.ShapeDtypeStruct((length, value_width), f32),
        jax.ShapeDtypeStruct((length, SUPER), f32),
        jax.ShapeDtypeStruct((length // BLOCK * key_width, value_width), f32),
        jax.ShapeDtypeStruct((length, value_width), f32),
    ]
    scratch = [pltpu.VMEM((length + 8, conv.shape[1]), f32)]
    return run_kernel(forward_kernel, out_shape, scratch, operands, 20_000_000_000)


def head_backward(operands, kept, grad_mixed):
    projected, small, conv, gain = operands[0], operands[1], operands[3], operands[6]
    f32 = jnp.float32
    out_shape = [
        jax.ShapeDtypeStruct(projected.shape, jnp.bfloat16),
        jax.ShapeDtypeStruct(small.shape, f32),
        jax.ShapeDtypeStruct(conv.shape, f32),
        jax.ShapeDtypeStruct((1, 1), f32),
        jax.ShapeDtypeStruct((1, 1), f32),
        jax.ShapeDtypeStruct(gain.shape, f32),
    ]
    scratch = [pltpu.VMEM((projected.shape[0] + 8, conv.shape[1]), f32)] * 2
    return run_kernel(
        backward_kernel, out_shape, scratch, (*operands, *kept, grad_mixed), 40_000_000_000
    )


def row_total(partial_rows):
    return lax.psum(partial_rows, "row")


def gather_tokens(block_rows):
    return lax.all_gather(block_rows, "col", axis=0, tiled=True)


def scatter_tokens(partial_rows):
    return lax.psum_scatter(
        partial_rows.astype(jnp.bfloat16), "col", scatter_dimension=0, tiled=True
    ).astype(jnp.float32)


def scatter_row(partial_rows):
    return lax.psum_scatter(
        partial_rows.astype(jnp.bfloat16), "row", scatter_dimension=0, tiled=True
    ).astype(jnp.float32)


def gather_row(rows):
    return lax.all_gather(rows, "row", axis=0, tiled=True)


def tie(*arrays):
    return lax.optimization_barrier(arrays)


def norm_forward(residual, gain_row, model_width):
    inverse = lax.rsqrt(row_total(jnp.sum(residual * residual, -1)) / model_width + norm_eps)
    scaled = residual * inverse[:, None]
    return (scaled * gain_row, scaled, inverse)


def norm_backward(grad_normed, scaled, inverse, gain_row, model_width):
    grad_scaled = grad_normed * gain_row
    inner_mean = row_total(jnp.sum(grad_scaled * scaled, -1)) / model_width
    grad_rows = inverse[:, None] * (grad_scaled - scaled * inner_mean[:, None])
    grad_gain = jnp.sum(grad_normed * scaled, 0)
    return (grad_rows, grad_gain)


def halving_total(part, order, size):
    index = lax.axis_index("dp")
    current = part
    for bit in order:
        upper = (index & bit) > 0
        half = current.shape[0] // 2
        low, high = current[:half], current[half:]
        away = jnp.where(upper, low, high).astype(jnp.bfloat16)
        stay = jnp.where(upper, high, low)
        came = lax.ppermute(away, "dp", [(i, i ^ bit) for i in range(size)])
        current = stay.astype(jnp.float32) + came.astype(jnp.float32)
    current = current.astype(jnp.bfloat16)
    for bit in reversed(order):
        upper = (index & bit) > 0
        came = lax.ppermute(current, "dp", [(i, i ^ bit) for i in range(size)])
        current = jnp.where(
            upper, jnp.concatenate([came, current], 0), jnp.concatenate([current, came], 0)
        )
    return current.astype(jnp.float32)


def dp_total(grad):
    size = lax.axis_size("dp")
    bits = [1 << place for place in range(size.bit_length() - 1)]
    half = grad.shape[0] // 2
    return jnp.concatenate(
        [halving_total(grad[:half], bits, size), halving_total(grad[half:], bits[::-1], size)], 0
    )


def body(
    inputs, norm_in, w_proj, w_small, w_conv, a_log, dt_bias, norm_out, w_out, norm_ffn,
    w_gu, w_down, block_resets, cotangent,
):
    row_width = norm_in.shape[1]
    row_size = lax.axis_size("row")
    col_size = lax.axis_size("col")
    model_width = row_width * row_size
    heads_col = w_proj.shape[2]
    heads_dev = heads_col // row_size
    row_index = lax.axis_index("row")
    col_index = lax.axis_index("col")
    head_first = row_index * heads_dev
    reset_tokens = jnp.repeat(block_flags(block_resets), BLOCK).astype(jnp.float32)[:, None]

    residual = inputs.astype(jnp.float32)
    normed, scaled_in, inverse_in = norm_forward(residual, norm_in[0], model_width)
    gathered_in = gather_tokens(normed.astype(jnp.bfloat16))
    length = gathered_in.shape[0]
    proj_part = jnp.einsum(
        "td,dhp->htp", gathered_in, w_proj[0], preferred_element_type=jnp.float32
    )
    small_part = jnp.einsum(
        "td,dhp->thp", gathered_in, w_small[0], preferred_element_type=jnp.float32
    )
    projected = scatter_row(proj_part)
    small_proj = lax.psum_scatter(small_part, "row", scatter_dimension=1, tiled=True)
    projected, cotangent_late = tie(projected, cotangent)
    conv_mine = lax.dynamic_slice_in_dim(w_conv[0], head_first, heads_dev, 1)
    alog_mine = lax.dynamic_slice_in_dim(a_log[0], head_first, heads_dev, 0)
    bias_mine = lax.dynamic_slice_in_dim(dt_bias[0], head_first, heads_dev, 0)
    head_args, head_kept, head_mixed = [], [], []
    for head in range(heads_dev):
        operands = (
            projected[head],
            small_proj[:, head],
            reset_tokens,
            conv_mine[:, head],
            alog_mine[head].reshape(1, 1),
            bias_mine[head].reshape(1, 1),
            norm_out,
        )
        mixed, *kept = head_forward(operands)
        head_args.append(operands)
        head_kept.append(kept)
        head_mixed.append(mixed)
    mixed_out = jnp.stack(head_mixed, 0)
    grad_branch = gather_tokens(cotangent_late)
    mixed_out, grad_branch = tie(mixed_out, grad_branch)
    gathered_heads = gather_row(mixed_out)
    branch = scatter_tokens(
        jnp.einsum("htv,hvd->td", gathered_heads, w_out[0], preferred_element_type=jnp.float32)
    )
    grad_hidden = scatter_row(
        jnp.einsum("td,fd->tf", grad_branch, w_down[0], preferred_element_type=jnp.float32)
    )
    middle = residual + branch
    normed_ffn, scaled_ffn, inverse_ffn = norm_forward(middle, norm_ffn[0], model_width)
    gathered_ffn = gather_tokens(normed_ffn.astype(jnp.bfloat16))
    gate_up = scatter_row(
        jnp.einsum("td,dkf->tkf", gathered_ffn, w_gu[0], preferred_element_type=jnp.float32)
    )
    gate_rows = gate_up[:, 0]
    up_rows = gate_up[:, 1]
    sigmoid_gate = jax.nn.sigmoid(gate_rows)
    hidden = (gate_rows * sigmoid_gate * up_rows).astype(jnp.bfloat16)
    grad_gate = grad_hidden * up_rows * sigmoid_gate * (1.0 + gate_rows * (1.0 - sigmoid_gate))
    grad_up = grad_hidden * gate_rows * sigmoid_gate
    grad_gate_up = gather_row(jnp.stack([grad_gate, grad_up], 1).astype(jnp.bfloat16))
    grad_normed_ffn = scatter_tokens(
        jnp.einsum("tkf,dkf->td", grad_gate_up, w_gu[0], preferred_element_type=jnp.float32)
    )
    hidden, _ = tie(hidden, grad_gate_up)
    hidden_all = gather_row(hidden)
    grad_down = jnp.einsum(
        "tf,td->fd", hidden_all, grad_branch, preferred_element_type=jnp.float32
    )
    grad_gu = jnp.einsum(
        "td,tkf->kfd", gathered_ffn, grad_gate_up, preferred_element_type=jnp.float32
    )
    total_down = dp_total(grad_down)
    total_gu = dp_total(grad_gu.reshape(-1, row_width))

    grad_middle, grad_gain_ffn = norm_backward(
        grad_normed_ffn, scaled_ffn, inverse_ffn, norm_ffn[0], model_width
    )
    grad_middle = cotangent.astype(jnp.float32) + grad_middle
    grad_middle_all = gather_tokens(grad_middle.astype(jnp.bfloat16))
    grad_mixed = lax.psum_scatter(
        jnp.einsum(
            "td,hvd->htv", grad_middle_all, w_out[0], preferred_element_type=jnp.float32
        ).astype(jnp.bfloat16),
        "row",
        scatter_dimension=0,
        tiled=True,
    )
    hidden_late, grad_mixed = tie(hidden_all, grad_mixed)
    last_branch = scatter_tokens(
        jnp.dot(hidden_late, w_down[0], preferred_element_type=jnp.float32)
    )
    result = (middle + last_branch).astype(jnp.bfloat16)
    grad_out = jnp.einsum(
        "htv,td->hvd", gathered_heads, grad_middle_all, preferred_element_type=jnp.float32
    )
    value_width = grad_out.shape[1]
    total_out = dp_total(grad_out.reshape(-1, row_width))

    backs = [
        head_backward(head_args[head], head_kept[head], grad_mixed[head])
        for head in range(heads_dev)
    ]
    grad_proj_mine = jnp.stack([back[0] for back in backs], 0)
    grad_small_mine = jnp.stack([back[1] for back in backs], 0).astype(jnp.bfloat16)
    grad_proj_all = gather_row(grad_proj_mine)
    grad_small_all = gather_row(grad_small_mine)
    grad_normed_in = scatter_tokens(
        jnp.einsum("htp,dhp->td", grad_proj_all, w_proj[0], preferred_element_type=jnp.float32)
        + jnp.einsum("htp,dhp->td", grad_small_all, w_small[0], preferred_element_type=jnp.float32)
    )
    grad_proj = jnp.einsum(
        "td,htp->hpd", gathered_in, grad_proj_all, preferred_element_type=jnp.float32
    )
    grad_small = jnp.einsum(
        "td,htp->hpd", gathered_in, grad_small_all, preferred_element_type=jnp.float32
    )
    proj_width = grad_proj.shape[1]
    total_proj = dp_total(grad_proj.reshape(-1, row_width))
    taps, channels = w_conv.shape[1], w_conv.shape[3]
    lanes = 128

    def padded_lanes(array):
        flat = array.reshape(-1)
        return jnp.pad(flat, (0, -flat.shape[0] % lanes)).reshape(-1, lanes)

    pieces = [
        padded_lanes(jnp.stack([back[2] for back in backs], 1)),
        padded_lanes(jnp.stack([back[3].reshape(()) for back in backs])),
        padded_lanes(jnp.stack([back[4].reshape(()) for back in backs])),
        padded_lanes(sum(back[5] for back in backs)),
        padded_lanes(grad_gain_ffn),
        padded_lanes(grad_small),
    ]
    starts = [0]
    for piece in pieces:
        starts.append(starts[-1] + piece.shape[0])
    summed = lax.psum(jnp.concatenate(pieces, 0), "dp")
    shared = lax.all_gather(summed[: starts[5]], ("col", "row"), axis=0, tiled=False)
    shared = shared.reshape(col_size, row_size, starts[5], lanes)
    mine = lax.dynamic_index_in_dim(shared, col_index, 0, keepdims=False)

    def taken(array, place, count):
        flat = array[..., starts[place] : starts[place + 1], :]
        return flat.reshape(flat.shape[:-2] + (-1,))[..., :count]

    conv_rows = taken(mine, 0, taps * heads_dev * channels).reshape(
        row_size, taps, heads_dev, channels
    )
    grad_conv = conv_rows.transpose(1, 0, 2, 3).reshape(1, taps, heads_col, channels)
    grad_alog = taken(mine, 1, heads_dev).reshape(1, heads_col)
    grad_bias = taken(mine, 2, heads_dev).reshape(1, heads_col)
    grad_norm_out = taken(shared, 3, value_width).sum((0, 1))[None]
    ffn_rows = taken(shared, 4, row_width).sum(0)
    grad_norm_ffn = lax.dynamic_slice_in_dim(ffn_rows, row_index, 1, 0)
    total_small = taken(summed, 5, grad_small.size).reshape(grad_small.shape)

    grad_in, grad_gain_in = norm_backward(
        grad_normed_in, scaled_in, inverse_in, norm_in[0], model_width
    )
    grad_rows = grad_middle + grad_in
    grad_norm_in = lax.psum(grad_gain_in, ("dp", "col"))[None]
    return (
        result,
        grad_rows,
        grad_norm_in,
        total_proj.reshape(heads_col, proj_width, row_width).transpose(2, 0, 1)[None],
        total_small.transpose(2, 0, 1)[None],
        grad_conv,
        grad_alog,
        grad_bias,
        grad_norm_out,
        total_out.reshape(heads_col, value_width, row_width)[None],
        grad_norm_ffn,
        total_gu.reshape(w_gu.shape[2], w_gu.shape[3], row_width).transpose(2, 0, 1)[None],
        total_down[None],
    )


def solution(mesh):
    in_specs = (
        P(("dp", "col"), "row"),
        P(None, "row"),
        P(None, "row", "col", None),
        P(None, "row", "col", None),
        P(None, None, "col", None),
        P(None, "col"),
        P(None, "col"),
        P(),
        P(None, "col", None, "row"),
        P(None, "row"),
        P(None, "row", None, "col"),
        P(None, "col", "row"),
        P("dp", None),
        P(("dp", "col"), "row"),
    )
    out_specs = (
        P(("dp", "col"), "row"),
        P(("dp", "col"), "row"),
        P(None, "row"),
        P(None, "row", "col", None),
        P(None, "row", "col", None),
        P(None, None, "col", None),
        P(None, "col"),
        P(None, "col"),
        P(),
        P(None, "col", None, "row"),
        P(None, "row"),
        P(None, "row", None, "col"),
        P(None, "col", "row"),
    )
    return jax.shard_map(body, mesh=mesh, in_specs=in_specs, out_specs=out_specs, check_vma=False)
```

```python
import jax
import jax.numpy as jnp
from jax import lax
from jax.experimental import pallas as pl
from jax.experimental.pallas import tpu as pltpu
from jax.sharding import PartitionSpec as P

BLOCK = 64
norm_eps = 1e-05
unit_eps = 1e-06


def block_flags(block_resets):
    column = lax.broadcasted_iota(jnp.int32, block_resets.shape, 1)
    return jnp.where(column == 0, 1, block_resets).reshape(-1)


SUPER = 256


def contract(left, right, left_dim, right_dim):
    dims = (((left_dim,), (right_dim,)), ((), ()))
    left_hi = left.astype(jnp.bfloat16)
    right_hi = right.astype(jnp.bfloat16)
    left_lo = (left - left_hi.astype(jnp.float32)).astype(jnp.bfloat16)
    right_lo = (right - right_hi.astype(jnp.float32)).astype(jnp.bfloat16)

    def single(one, other):
        return lax.dot_general(one, other, dims, preferred_element_type=jnp.float32)

    return single(left_hi, right_hi) + (single(left_hi, right_lo) + single(left_lo, right_hi))


@jax.custom_vjp
def nn(left, right):
    return contract(left, right, 1, 0)


@jax.custom_vjp
def nt(left, right):
    return contract(left, right, 1, 1)


@jax.custom_vjp
def tn(left, right):
    return contract(left, right, 0, 0)


nn.defvjp(lambda a, b: (nn(a, b), (a, b)), lambda k, g: (nt(g, k[1]), tn(k[0], g)))
nt.defvjp(lambda a, b: (nt(a, b), (a, b)), lambda k, g: (nn(g, k[1]), tn(g, k[0])))
tn.defvjp(lambda a, b: (tn(a, b), (a, b)), lambda k, g: (nt(k[1], g), nn(k[0], g)))


@jax.custom_vjp
def solve(inverse, coupling, targets):
    return nn(inverse, targets)


def solve_fwd(inverse, coupling, targets):
    solved = nn(inverse, targets)
    return solved, (inverse, solved)


def solve_bwd(kept, grad):
    inverse, solved = kept
    grad_targets = tn(inverse, grad)
    return jnp.zeros_like(inverse), -nt(grad_targets, solved), grad_targets


solve.defvjp(solve_fwd, solve_bwd)


def block_masks():
    rows = lax.broadcasted_iota(jnp.int32, (SUPER, SUPER), 0)
    cols = lax.broadcasted_iota(jnp.int32, (SUPER, SUPER), 1)
    shift = BLOCK.bit_length() - 1
    same = (rows >> shift) == (cols >> shift)
    return rows, cols, same


def unit_lower_inverse(coupling, rows, cols):
    eye = jnp.where(rows == cols, 1.0, 0.0)
    inverse = None
    for level in range(BLOCK.bit_length() - 1):
        pair = ((rows >> (level + 1)) == (cols >> (level + 1))) & (
            ((rows >> level) & 1) > ((cols >> level) & 1)
        )
        corner = jnp.where(pair, coupling, 0.0)
        if inverse is None:
            inverse = eye - corner
        else:
            inverse = inverse - nn(nn(inverse, corner), inverse)
    return inverse


def intra(query_act, key_act, values, beta, log_decay, inverse, masks):
    rows, cols, same = masks
    key_width = query_act.shape[1]
    queries = (
        query_act
        * lax.rsqrt(jnp.sum(query_act * query_act, -1, keepdims=True) + unit_eps)
        * key_width ** (-0.5)
    )
    keys_all = key_act * lax.rsqrt(jnp.sum(key_act * key_act, -1, keepdims=True) + unit_eps)
    eye = jnp.where(rows == cols, 1.0, 0.0)
    upto = jnp.where(same & (rows <= cols), 1.0, 0.0)
    sames = jnp.where(same, 1.0, 0.0)
    lower = same & (rows >= cols)
    strict = same & (rows > cols)
    cum_row = jnp.sum(log_decay * upto, 0, keepdims=True)
    total_row = jnp.sum(log_decay * sames, 0, keepdims=True)
    cum = jnp.sum(cum_row * eye, 1, keepdims=True)
    total = jnp.sum(total_row * eye, 1, keepdims=True)
    decays = jnp.exp(cum)
    within = jnp.where(lower, jnp.exp(jnp.where(lower, cum - cum_row, 0.0)), 0.0)
    coupling = jnp.where(strict, beta * nt(keys_all, keys_all) * within, 0.0)
    if inverse is None:
        inverse = unit_lower_inverse(coupling, rows, cols)
    solved_v = solve(inverse, coupling, beta * values)
    solved_k = solve(inverse, coupling, (beta * decays) * keys_all)
    scores = nt(queries, keys_all) * within
    return (
        solved_v,
        solved_k,
        scores,
        queries * decays,
        keys_all * jnp.exp(total - cum),
        jnp.exp(total),
    ), inverse


def gated(output, gate, gain):
    scaled = output * lax.rsqrt(jnp.mean(output * output, -1, keepdims=True) + norm_eps)
    return scaled * gain * (gate * lax.logistic(gate))


def gates(small, a_log, dt_bias):
    beta = lax.logistic(small[:, 0:1])
    shifted = small[:, 1:2] + dt_bias
    soft = jnp.maximum(shifted, 0.0) + jnp.log1p(jnp.exp(-jnp.abs(shifted)))
    return beta, -jnp.exp(a_log) * soft, shifted


def fill_padded(padded, projected_ref, channels):
    padded[0:8, :] = jnp.zeros((8, channels), jnp.float32)
    padded[8:, :] = projected_ref[:, :channels]


def taps_kept(reset_rows, offset):
    place = lax.broadcasted_iota(jnp.int32, reset_rows.shape, 0) & (BLOCK - 1)
    return jnp.where(place < offset, 1.0 - reset_rows, 1.0)


def convolve(padded, conv_ref, reset_rows, first):
    summed = None
    for offset in range(conv_ref.shape[0]):
        term = conv_ref[offset : offset + 1, :] * padded[pl.ds(8 + first - offset, SUPER), :]
        if offset:
            term = term * taps_kept(reset_rows, offset)
        summed = term if summed is None else summed + term
    return summed


def forward_kernel(
    projected_ref, small_ref, reset_ref, conv_ref, alog_ref, bias_ref, gain_ref,
    mixed_ref, output_ref, inverse_ref, state_ref, update_ref, padded,
):
    length = projected_ref.shape[0]
    channels = conv_ref.shape[1]
    value_width = gain_ref.shape[1]
    key_width = (channels - value_width) // 2
    masks = block_masks()
    fill_padded(padded, projected_ref, channels)
    pieces = []
    for first in range(0, length, SUPER):
        span = slice(first, first + SUPER)
        summed = convolve(padded, conv_ref, reset_ref[span, :], first)
        act = summed * lax.logistic(summed)
        beta, log_decay, _ = gates(small_ref[span, :], alog_ref[...], bias_ref[...])
        made, inverse = intra(
            act[:, :key_width], act[:, key_width : 2 * key_width], act[:, 2 * key_width :],
            beta, log_decay, None, masks,
        )
        inverse_ref[span, :] = inverse
        pieces.append(made)
    state = jnp.zeros((key_width, value_width), jnp.float32)
    for index, first in enumerate(range(0, length, SUPER)):
        solved_v, solved_k, scores, query_decay, key_rest, last = pieces[index]
        updates, reads = [], []
        for start in range(0, SUPER, BLOCK):
            part = slice(start, start + BLOCK)
            block = (first + start) // BLOCK
            reset_now = reset_ref[first + start : first + start + 1, :]
            state = state * (1.0 - reset_now)
            state_ref[block * key_width : (block + 1) * key_width, :] = state
            transfer = tn(key_rest[part], solved_k[part])
            added = tn(key_rest[part], solved_v[part])
            updates.append(solved_v[part] - nn(solved_k[part], state))
            reads.append(nn(query_decay[part], state))
            state = last[start : start + 1, :] * state + added - nn(transfer, state)
        update = jnp.concatenate(updates, 0)
        output = jnp.concatenate(reads, 0) + nn(scores, update)
        span = slice(first, first + SUPER)
        update_ref[span, :] = update
        output_ref[span, :] = output
        mixed_ref[span, :] = gated(output, projected_ref[span, channels:], gain_ref[...]).astype(
            mixed_ref.dtype
        )


def backward_kernel(
    projected_ref, small_ref, reset_ref, conv_ref, alog_ref, bias_ref, gain_ref,
    output_ref, inverse_ref, state_ref, update_ref, grad_ref,
    dproj_ref, dsmall_ref, dconv_ref, dalog_ref, dbias_ref, dgain_ref, padded, dpadded,
):
    length = projected_ref.shape[0]
    channels = conv_ref.shape[1]
    value_width = gain_ref.shape[1]
    key_width = (channels - value_width) // 2
    tap_count = conv_ref.shape[0]
    masks = block_masks()
    fill_padded(padded, projected_ref, channels)
    dpadded[length:, :] = jnp.zeros((8, channels), jnp.float32)
    dstate = jnp.zeros((key_width, value_width), jnp.float32)
    dgain = jnp.zeros((1, value_width), jnp.float32)
    dalog = jnp.zeros((1, 1), jnp.float32)
    dbias = jnp.zeros((1, 1), jnp.float32)
    dconv = [jnp.zeros((1, channels), jnp.float32) for _ in range(tap_count)]
    for first in reversed(range(0, length, SUPER)):
        span = slice(first, first + SUPER)
        _, pull_gated = jax.vjp(
            gated, output_ref[span, :], projected_ref[span, channels:], gain_ref[...]
        )
        doutput, dgate, dgain_part = pull_gated(grad_ref[span, :].astype(jnp.float32))
        dgain = dgain + dgain_part
        dproj_ref[span, channels:] = dgate.astype(dproj_ref.dtype)
        summed = convolve(padded, conv_ref, reset_ref[span, :], first)
        gate_of = lax.logistic(summed)
        act = summed * gate_of
        beta, log_decay, shifted = gates(small_ref[span, :], alog_ref[...], bias_ref[...])
        inverse = inverse_ref[span, :]
        made, pull_intra = jax.vjp(
            lambda q, k, v, b, g: intra(q, k, v, b, g, inverse, masks)[0],
            act[:, :key_width], act[:, key_width : 2 * key_width], act[:, 2 * key_width :],
            beta, log_decay,
        )
        _, solved_k, scores, query_decay, key_rest, last = made
        update = update_ref[span, :]
        dscores = nt(doutput, update)
        through = tn(scores, doutput)
        dupdates, dsolved_k, dquery, dkey, dlast = [], [], [], [], []
        for start in reversed(range(0, SUPER, BLOCK)):
            part = slice(start, start + BLOCK)
            block = (first + start) // BLOCK
            reset_now = reset_ref[first + start : first + start + 1, :]
            state = state_ref[block * key_width : (block + 1) * key_width, :]
            last_now = last[start : start + 1, :]
            transfer = tn(solved_k[part], key_rest[part])
            given = tn(query_decay[part], doutput[part]) - tn(solved_k[part], through[part])
            dupdate = through[part] + nn(key_rest[part], dstate)
            dupdates.append(dupdate)
            dsolved_k.append(-nt(dupdate, state))
            dquery.append(nt(doutput[part], state))
            dkey.append(nt(update[part], dstate))
            inner = jnp.sum(
                jnp.sum(state * dstate, 1, keepdims=True), 0, keepdims=True
            )
            place = lax.broadcasted_iota(jnp.int32, (BLOCK, 1), 0)
            dlast.append(jnp.where(place == 0, inner, 0.0))
            dstate = (last_now * dstate + given - nn(transfer, dstate)) * (1.0 - reset_now)
        joined = [jnp.concatenate(p[::-1], 0) for p in (dupdates, dsolved_k, dquery, dkey, dlast)]
        dq, dk, dv, dbeta, dlog = pull_intra(
            (joined[0], joined[1], dscores, joined[2], joined[3], joined[4])
        )
        dsmall_ref[span, 0:1] = dbeta * beta * (1.0 - beta)
        dshift = dlog * (-jnp.exp(alog_ref[...])) * lax.logistic(shifted)
        dsmall_ref[span, 1:2] = dshift
        dalog = dalog + jnp.sum(dlog * log_decay, 0, keepdims=True)
        dbias = dbias + jnp.sum(dshift, 0, keepdims=True)
        slope = gate_of * (1.0 + summed * (1.0 - gate_of))
        dpadded[span, :] = jnp.concatenate([dq, dk, dv], 1) * slope
    for first in range(0, length, SUPER):
        span = slice(first, first + SUPER)
        here = dpadded[span, :]
        total = conv_ref[0:1, :] * here
        dconv[0] = dconv[0] + jnp.sum(here * padded[pl.ds(8 + first, SUPER), :], 0, keepdims=True)
        place = lax.broadcasted_iota(jnp.int32, (SUPER, 1), 0)
        at_last = place >= SUPER - 8
        for offset in range(1, tap_count):
            back = padded[pl.ds(8 + first - offset, SUPER), :] * taps_kept(reset_ref[span, :], offset)
            dconv[offset] = dconv[offset] + jnp.sum(here * back, 0, keepdims=True)
            ahead = dpadded[pl.ds(first + offset, SUPER), :]
            kept = next_kept(reset_ref, first, length, offset)
            total = total + conv_ref[offset : offset + 1, :] * (ahead * kept)
        dproj_ref[span, :channels] = total.astype(dproj_ref.dtype)
    for offset in range(tap_count):
        dconv_ref[offset : offset + 1, :] = dconv[offset]
    dalog_ref[...] = dalog
    dbias_ref[...] = dbias
    dgain_ref[...] = dgain


def next_kept(reset_ref, first, length, offset):
    place = lax.broadcasted_iota(jnp.int32, (BLOCK, 1), 0)
    kept = []
    for start in range(first, first + SUPER, BLOCK):
        if start + BLOCK < length:
            after = 1.0 - reset_ref[start + BLOCK : start + 2 * BLOCK, :]
        else:
            after = jnp.zeros((BLOCK, 1), jnp.float32)
        kept.append(jnp.where(place + offset >= BLOCK, after, 1.0))
    return jnp.concatenate(kept, 0)


vmem_limit = 60 * 1024 * 1024


def run_kernel(kernel, out_shape, scratch, operands, cost):
    return pl.pallas_call(
        kernel,
        out_shape=out_shape,
        in_specs=[pl.BlockSpec(memory_space=pltpu.VMEM)] * len(operands),
        out_specs=[pl.BlockSpec(memory_space=pltpu.VMEM)] * len(out_shape),
        scratch_shapes=scratch,
        compiler_params=pltpu.CompilerParams(vmem_limit_bytes=vmem_limit),
        cost_estimate=pl.CostEstimate(flops=cost, bytes_accessed=8_000_000, transcendentals=1_000_000),
    )(*operands)


def head_forward(operands):
    projected, conv, gain = operands[0], operands[3], operands[6]
    length, value_width = projected.shape[0], gain.shape[1]
    key_width = (conv.shape[1] - value_width) // 2
    f32 = jnp.float32
    out_shape = [
        jax.ShapeDtypeStruct((length, value_width), jnp.bfloat16),
        jax.ShapeDtypeStruct((length, value_width), f32),
        jax.ShapeDtypeStruct((length, SUPER), f32),
        jax.ShapeDtypeStruct((length // BLOCK * key_width, value_width), f32),
        jax.ShapeDtypeStruct((length, value_width), f32),
    ]
    scratch = [pltpu.VMEM((length + 8, conv.shape[1]), f32)]
    return run_kernel(forward_kernel, out_shape, scratch, operands, 20_000_000_000)


def head_backward(operands, kept, grad_mixed):
    projected, small, conv, gain = operands[0], operands[1], operands[3], operands[6]
    f32 = jnp.float32
    out_shape = [
        jax.ShapeDtypeStruct(projected.shape, jnp.bfloat16),
        jax.ShapeDtypeStruct(small.shape, f32),
        jax.ShapeDtypeStruct(conv.shape, f32),
        jax.ShapeDtypeStruct((1, 1), f32),
        jax.ShapeDtypeStruct((1, 1), f32),
        jax.ShapeDtypeStruct(gain.shape, f32),
    ]
    scratch = [pltpu.VMEM((projected.shape[0] + 8, conv.shape[1]), f32)] * 2
    return run_kernel(
        backward_kernel, out_shape, scratch, (*operands, *kept, grad_mixed), 40_000_000_000
    )


def row_total(partial_rows):
    return lax.psum(partial_rows, "row")


def gather_tokens(block_rows):
    return lax.all_gather(block_rows, "col", axis=0, tiled=True)


def scatter_tokens(partial_rows):
    return lax.psum_scatter(
        partial_rows.astype(jnp.bfloat16), "col", scatter_dimension=0, tiled=True
    ).astype(jnp.float32)


def swap_row(array):
    return lax.ppermute(array, "row", [(0, 1), (1, 0)])


def own_half(array, index, axis=0):
    half = array.shape[axis] // 2
    return lax.dynamic_slice_in_dim(array, index * half, half, axis)


def scatter_row(partial_of, index):
    came = swap_row(partial_of(1 - index).astype(jnp.bfloat16))
    return partial_of(index) + came.astype(jnp.float32)


def gather_row(rows, index):
    came = swap_row(rows)
    return jnp.where(
        index > 0, jnp.concatenate([came, rows], 0), jnp.concatenate([rows, came], 0)
    )


def spread_total(array, axis_name):
    size = lax.axis_size(axis_name)
    step = 1
    while step < size:
        count = min(4, size // step)
        came = [array] + [
            lax.ppermute(array, axis_name, [(i, i ^ (step * k)) for i in range(size)])
            for k in range(1, count)
        ]
        array = came[0] + came[1]
        if count == 4:
            array = array + (came[2] + came[3])
        step *= count
    return array


def tie(*arrays):
    return lax.optimization_barrier(arrays)


def norm_forward(residual, gain_row, model_width):
    inverse = lax.rsqrt(row_total(jnp.sum(residual * residual, -1)) / model_width + norm_eps)
    scaled = residual * inverse[:, None]
    return (scaled * gain_row, scaled, inverse)


def norm_backward(grad_normed, scaled, inverse, gain_row, model_width):
    grad_scaled = grad_normed * gain_row
    inner_mean = row_total(jnp.sum(grad_scaled * scaled, -1)) / model_width
    grad_rows = inverse[:, None] * (grad_scaled - scaled * inner_mean[:, None])
    grad_gain = jnp.sum(grad_normed * scaled, 0)
    return (grad_rows, grad_gain)


def halving_total(part, order, size):
    index = lax.axis_index("dp")
    current = part
    for bit in order:
        upper = (index & bit) > 0
        half = current.shape[0] // 2
        low, high = current[:half], current[half:]
        away = jnp.where(upper, low, high).astype(jnp.bfloat16)
        stay = jnp.where(upper, high, low)
        came = lax.ppermute(away, "dp", [(i, i ^ bit) for i in range(size)])
        current = stay.astype(jnp.float32) + came.astype(jnp.float32)
    current = current.astype(jnp.bfloat16)
    for bit in reversed(order):
        upper = (index & bit) > 0
        came = lax.ppermute(current, "dp", [(i, i ^ bit) for i in range(size)])
        current = jnp.where(
            upper, jnp.concatenate([came, current], 0), jnp.concatenate([current, came], 0)
        )
    return current.astype(jnp.float32)


def dp_total(grad):
    size = lax.axis_size("dp")
    bits = [1 << place for place in range(size.bit_length() - 1)]
    half = grad.shape[0] // 2
    return jnp.concatenate(
        [halving_total(grad[:half], bits, size), halving_total(grad[half:], bits[::-1], size)], 0
    )


def body(
    inputs, norm_in, w_proj, w_small, w_conv, a_log, dt_bias, norm_out, w_out, norm_ffn,
    w_gu, w_down, block_resets, cotangent,
):
    row_width = norm_in.shape[1]
    row_size = lax.axis_size("row")
    col_size = lax.axis_size("col")
    model_width = row_width * row_size
    heads_col = w_proj.shape[2]
    heads_dev = heads_col // row_size
    row_index = lax.axis_index("row")
    col_index = lax.axis_index("col")
    head_first = row_index * heads_dev
    reset_tokens = jnp.repeat(block_flags(block_resets), BLOCK).astype(jnp.float32)[:, None]

    residual = inputs.astype(jnp.float32)
    normed, scaled_in, inverse_in = norm_forward(residual, norm_in[0], model_width)
    gathered_in = gather_tokens(normed.astype(jnp.bfloat16))
    length = gathered_in.shape[0]

    def proj_part(index):
        return jnp.einsum(
            "td,dhp->htp", gathered_in, own_half(w_proj[0], index, 1),
            preferred_element_type=jnp.float32,
        )

    small_part = jnp.einsum(
        "td,dhp->htp", gathered_in, w_small[0], preferred_element_type=jnp.float32
    )
    projected = scatter_row(proj_part, row_index)
    small_proj = own_half(small_part, row_index) + swap_row(own_half(small_part, 1 - row_index))
    projected, cotangent_late = tie(projected, cotangent)
    conv_mine = lax.dynamic_slice_in_dim(w_conv[0], head_first, heads_dev, 1)
    alog_mine = lax.dynamic_slice_in_dim(a_log[0], head_first, heads_dev, 0)
    bias_mine = lax.dynamic_slice_in_dim(dt_bias[0], head_first, heads_dev, 0)
    head_args, head_kept, head_mixed = [], [], []
    for head in range(heads_dev):
        operands = (
            projected[head],
            small_proj[head],
            reset_tokens,
            conv_mine[:, head],
            alog_mine[head].reshape(1, 1),
            bias_mine[head].reshape(1, 1),
            norm_out,
        )
        mixed, *kept = head_forward(operands)
        head_args.append(operands)
        head_kept.append(kept)
        head_mixed.append(mixed)
    mixed_out = jnp.stack(head_mixed, 0)
    grad_branch = gather_tokens(cotangent_late)
    mixed_out, grad_branch = tie(mixed_out, grad_branch)
    mixed_came = swap_row(mixed_out)

    def out_part(heads, index):
        return jnp.einsum(
            "htv,hvd->td", heads, own_half(w_out[0], index), preferred_element_type=jnp.float32
        )

    branch_part = out_part(mixed_out, row_index) + out_part(mixed_came, 1 - row_index)
    branch = scatter_tokens(branch_part)
    gathered_heads = jnp.where(
        row_index > 0,
        jnp.concatenate([mixed_came, mixed_out], 0),
        jnp.concatenate([mixed_out, mixed_came], 0),
    )
    branch_part, grad_branch_late = tie(branch_part, grad_branch)
    grad_hidden = scatter_row(
        lambda index: jnp.einsum(
            "td,fd->tf", own_half(grad_branch_late, index), w_down[0],
            preferred_element_type=jnp.float32,
        ),
        row_index,
    )
    branch, grad_hidden = tie(branch, grad_hidden)
    middle = residual + branch
    normed_ffn, scaled_ffn, inverse_ffn = norm_forward(middle, norm_ffn[0], model_width)
    gathered_ffn = gather_tokens(normed_ffn.astype(jnp.bfloat16))
    gate_up = scatter_row(
        lambda index: jnp.einsum(
            "td,dkf->ktf", own_half(gathered_ffn, index), w_gu[0],
            preferred_element_type=jnp.float32,
        ),
        row_index,
    )
    gate_rows, up_rows = gate_up[0], gate_up[1]
    sigmoid_gate = jax.nn.sigmoid(gate_rows)
    hidden = (gate_rows * sigmoid_gate * up_rows).astype(jnp.bfloat16)
    grad_gate = grad_hidden * up_rows * sigmoid_gate * (1.0 + gate_rows * (1.0 - sigmoid_gate))
    grad_up = grad_hidden * gate_rows * sigmoid_gate
    grad_gate_all = gather_row(grad_gate.astype(jnp.bfloat16), row_index)
    grad_up_all = gather_row(grad_up.astype(jnp.bfloat16), row_index)
    ffn_part = (
        jnp.einsum("tf,df->td", grad_gate_all, w_gu[0][:, 0], preferred_element_type=jnp.float32)
        + jnp.einsum("tf,df->td", grad_up_all, w_gu[0][:, 1], preferred_element_type=jnp.float32)
    ).astype(jnp.bfloat16)
    grad_normed_ffn = scatter_tokens(ffn_part)
    hidden, grad_gate_all, grad_up_all, _ = tie(hidden, grad_gate_all, grad_up_all, ffn_part)
    hidden_all = gather_row(hidden, row_index)
    grad_down = jnp.einsum(
        "tf,td->fd", hidden_all, grad_branch, preferred_element_type=jnp.float32
    )
    ffn_group = jnp.concatenate(
        [
            jnp.einsum("tf,td->fd", grad_gate_all, gathered_ffn, preferred_element_type=jnp.float32),
            jnp.einsum("tf,td->fd", grad_up_all, gathered_ffn, preferred_element_type=jnp.float32),
            grad_down,
        ],
        0,
    ).astype(jnp.bfloat16)
    grad_normed_ffn, ffn_group = tie(grad_normed_ffn, ffn_group)
    total_ffn = dp_total(ffn_group)
    hidden_units = w_down.shape[1]
    total_gu = total_ffn[: 2 * hidden_units]
    total_down = total_ffn[2 * hidden_units :]

    grad_middle, grad_gain_ffn = norm_backward(
        grad_normed_ffn, scaled_ffn, inverse_ffn, norm_ffn[0], model_width
    )
    grad_middle = cotangent.astype(jnp.float32) + grad_middle
    grad_middle_all = gather_tokens(grad_middle.astype(jnp.bfloat16))
    grad_mixed = scatter_row(
        lambda index: jnp.einsum(
            "td,hvd->htv", grad_middle_all, own_half(w_out[0], index),
            preferred_element_type=jnp.float32,
        ),
        row_index,
    )
    hidden_late, grad_mixed = tie(hidden_all, grad_mixed)
    last_branch = scatter_tokens(
        jnp.dot(hidden_late, w_down[0], preferred_element_type=jnp.float32)
    )
    result = (middle + last_branch).astype(jnp.bfloat16)
    grad_out = jnp.einsum(
        "htv,td->hvd", gathered_heads, grad_middle_all, preferred_element_type=jnp.float32
    )
    value_width = grad_out.shape[1]
    backs = [
        head_backward(head_args[head], head_kept[head], grad_mixed[head])
        for head in range(heads_dev)
    ]
    grad_proj_mine = jnp.stack([back[0] for back in backs], 0)
    grad_small_mine = jnp.stack([back[1] for back in backs], 0).astype(jnp.bfloat16)
    proj_came = swap_row(grad_proj_mine)
    grad_small_all = gather_row(grad_small_mine, row_index)

    def in_part(heads, index):
        return jnp.einsum(
            "htp,dhp->td", heads, own_half(w_proj[0], index, 1), preferred_element_type=jnp.float32
        )

    in_partial = (
        in_part(grad_proj_mine, row_index)
        + in_part(proj_came, 1 - row_index)
        + jnp.einsum("htp,dhp->td", grad_small_all, w_small[0], preferred_element_type=jnp.float32)
    ).astype(jnp.bfloat16)
    grad_normed_in = scatter_tokens(in_partial)
    grad_proj_all = jnp.where(
        row_index > 0,
        jnp.concatenate([proj_came, grad_proj_mine], 0),
        jnp.concatenate([grad_proj_mine, proj_came], 0),
    )
    grad_proj = jnp.einsum(
        "td,htp->hpd", gathered_in, grad_proj_all, preferred_element_type=jnp.float32
    )
    grad_small = jnp.einsum(
        "td,htp->hpd", gathered_in, grad_small_all, preferred_element_type=jnp.float32
    )
    proj_width = grad_proj.shape[1]
    mixer_group = jnp.concatenate(
        [grad_proj.reshape(-1, row_width), grad_out.reshape(-1, row_width)], 0
    ).astype(jnp.bfloat16)
    mixer_group, grad_small = tie(mixer_group, grad_small)
    total_mixer = dp_total(mixer_group)
    total_proj = total_mixer[: heads_col * proj_width]
    total_out = total_mixer[heads_col * proj_width :]
    taps, channels = w_conv.shape[1], w_conv.shape[3]
    lanes = 128

    def padded_lanes(array):
        flat = array.reshape(-1)
        return jnp.pad(flat, (0, -flat.shape[0] % lanes)).reshape(-1, lanes)

    pieces = [
        padded_lanes(jnp.stack([back[2] for back in backs], 1)),
        padded_lanes(jnp.stack([back[3].reshape(()) for back in backs])),
        padded_lanes(jnp.stack([back[4].reshape(()) for back in backs])),
        padded_lanes(grad_small),
        padded_lanes(sum(back[5] for back in backs)),
        padded_lanes(grad_gain_ffn),
    ]
    starts = [0]
    for piece in pieces:
        starts.append(starts[-1] + piece.shape[0])
    summed = spread_total(jnp.concatenate(pieces, 0), "dp")
    gains = spread_total(summed[starts[4] :], "col")
    gain_rows = starts[5] - starts[4]
    near = jnp.concatenate([summed[: starts[3]], gains[:gain_rows]], 0)
    far = swap_row(near)

    def taken(array, first, count):
        return array[first:].reshape(-1)[:count]

    def both(first, shape):
        count = 1
        for extent in shape:
            count *= extent
        mine = taken(near, first, count).reshape(shape)
        other = taken(far, first, count).reshape(shape)
        return jnp.where(
            row_index > 0,
            jnp.concatenate([other, mine], -1 if len(shape) == 1 else 1),
            jnp.concatenate([mine, other], -1 if len(shape) == 1 else 1),
        )[None]

    grad_conv = both(starts[0], (taps, heads_dev, channels))
    grad_alog = both(starts[1], (heads_dev,))
    grad_bias = both(starts[2], (heads_dev,))
    grad_norm_out = taken(near + far, starts[3], value_width)[None]
    grad_norm_ffn = taken(gains, gain_rows, row_width)[None]
    total_small = taken(summed, starts[3], grad_small.size).reshape(grad_small.shape)

    grad_in, grad_gain_in = norm_backward(
        grad_normed_in, scaled_in, inverse_in, norm_in[0], model_width
    )
    grad_rows = grad_middle + grad_in
    grad_norm_in = spread_total(spread_total(padded_lanes(grad_gain_in), "dp"), "col")
    grad_norm_in = grad_norm_in.reshape(1, -1)[:, :row_width]
    return (
        result,
        grad_rows,
        grad_norm_in,
        total_proj.reshape(heads_col, proj_width, row_width).transpose(2, 0, 1)[None],
        total_small.transpose(2, 0, 1)[None],
        grad_conv,
        grad_alog,
        grad_bias,
        grad_norm_out,
        total_out.reshape(heads_col, value_width, row_width)[None],
        grad_norm_ffn,
        total_gu.reshape(w_gu.shape[2], w_gu.shape[3], row_width).transpose(2, 0, 1)[None],
        total_down[None],
    )


def solution(mesh):
    in_specs = (
        P(("dp", "col"), "row"),
        P(None, "row"),
        P(None, "row", "col", None),
        P(None, "row", "col", None),
        P(None, None, "col", None),
        P(None, "col"),
        P(None, "col"),
        P(),
        P(None, "col", None, "row"),
        P(None, "row"),
        P(None, "row", None, "col"),
        P(None, "col", "row"),
        P("dp", None),
        P(("dp", "col"), "row"),
    )
    out_specs = (
        P(("dp", "col"), "row"),
        P(("dp", "col"), "row"),
        P(None, "row"),
        P(None, "row", "col", None),
        P(None, "row", "col", None),
        P(None, None, "col", None),
        P(None, "col"),
        P(None, "col"),
        P(),
        P(None, "col", None, "row"),
        P(None, "row"),
        P(None, "row", None, "col"),
        P(None, "col", "row"),
    )
    return jax.shard_map(body, mesh=mesh, in_specs=in_specs, out_specs=out_specs, check_vma=False)
```
